32 devices in a mesh: ens: 2 (over y), bfly: 4 (over z), cblk: 4 (over x, core).
Axes of the slice: x: 2, y: 2, z: 4, core: 2. Of those that a mesh axis runs over, the one named last changes fastest.
Arguments:
- source: bfloat16 [65536, 512], P(('ens', 'bfly', 'cblk')), parts along dimension 0, may hold values from -6 to 6
- basis: bfloat16 [65536, 256], P(('ens', 'bfly', 'cblk')), parts along dimension 0, may hold values from -0.0625 to 0.0625
- transfer: bfloat16 [4, 4, 256, 512], P('ens', 'bfly'), parts along dimension 0, may hold values from -0.25 to 0.25
- skeleton: int32 [32, 16], P(('ens', 'bfly', 'cblk')), parts along dimension 0, may hold values from 0 to 15, each once within a row
- row_class: int32 [65536], P(('ens', 'bfly', 'cblk')), parts along dimension 0, may hold values from 0 to 15
- linear_table: float32 [16, 512], replicated, may hold values from 0.5 to 1.5
- cubic_table: float32 [16, 512], replicated, may hold values from 0.05 to 0.3
Outputs:
- adjoint: bfloat16 [65536, 512], P(('ens', 'bfly', 'cblk')), parts along dimension 0
The draws below stay inside these ranges and needn't reach their ends.
There are 2 independent parts, one for each index of `ens`. The reference program is written for one: setup_inputs(seed, part) draws one part's arguments, and reference() takes and returns one part's arrays. A program takes and returns all parts, laid end to end along the dimension named above; an argument that names none is the same for every part. Nothing has to cross between parts.
Inputs may be any that keep to these rules, and one draw needn't show every extreme that they name: Each row of skeleton names each of the 16 tiles once.
All inputs are finite; a program needn't handle non-finite values.
Results may differ from the reference program's by a relative error of at most 0.0052.
Values may be sent and summed in bfloat16 or wider, within the bound.
A program may use at most 64 MiB of HBM per device.

```python
import math
import jax
import jax.numpy as jnp
import numpy as np
from jax import lax

R = 256
C = 512
TILE = 128
KTAB = 16
TILES = 16
ROWS_BLK = 8192
ROWS = 32768
LEVELS = 2
N_BFLY = 4
N_CBLK = 4


def with_ends(result, rng, low, high):
    longest = result.shape.index(max(result.shape))
    spots = []
    for shift in (0, 1):
        where = [jax.random.randint(jax.random.fold_in(rng, axis), (), 0, length) for axis, length in enumerate(result.shape)]
        where[longest] = (where[longest] + shift) % result.shape[longest]
        spots.append(tuple(where))
    return result.at[spots[0]].set(low).at[spots[1]].set(high)


def block_levels(own_key, shape, cuts, low, top_value):
    level, own = 1.0, jax.random.fold_in(own_key, 6)
    for axis_at, blocks in cuts:
        steps = jnp.exp(jax.random.uniform(jax.random.fold_in(own, axis_at), (blocks,), jnp.float32, low / len(cuts), top_value / len(cuts)))
        level = level * jnp.repeat(steps, shape[axis_at] // blocks).reshape([-1 if axis == axis_at else 1 for axis in range(len(shape))])
    return level


def normal_values(rng, extent, width, reach, pieces=(), dtype=jnp.bfloat16):
    values = width * jax.random.normal(rng, extent, jnp.float32)
    if pieces:
        values = values * block_levels(rng, extent, pieces, -0.22, 0.18)
    return jnp.clip(values, -reach, reach).astype(dtype)


def setup_inputs(seed: int = 0, part: int = 0) -> dict:
    streams_of = jax.random.split(jax.random.key(seed), 8)
    part_splits = jax.random.split(jax.random.fold_in(streams_of[7], part), 8)
    return {
        "source": normal_values(part_splits[0], (ROWS, C), 1.0, 6.0, ((0, 16),)),
        "basis": normal_values(part_splits[1], (ROWS, R), ROWS_BLK ** -0.5, 0.0625, ((0, 16),)),
        "transfer": normal_values(part_splits[2], (LEVELS, N_BFLY, R, 2 * R), (2 * R) ** -0.5, 0.25, ((1, 4),)),
        "skeleton": jax.vmap(lambda own: jax.random.permutation(own, TILES))(jax.random.split(part_splits[3], (N_BFLY * N_CBLK))).reshape((N_BFLY * N_CBLK, TILES)).astype(jnp.int32),
        "row_class": with_ends(jax.random.randint(part_splits[4], (ROWS,), 0, KTAB), jax.random.fold_in(part_splits[4], 1), 0, KTAB - 1).astype(jnp.int32),
        "linear_table": jnp.clip(jax.random.uniform(streams_of[5], (KTAB, C), jnp.float32, 0.5, 1.5), 0.5, 1.5),
        "cubic_table": jnp.clip(jax.random.uniform(streams_of[6], (KTAB, C), jnp.float32, 0.05, 0.3), 0.05, 0.3),
    }


def reference(source, basis, transfer, skeleton, row_class, linear_table, cubic_table):
    highest = lax.Precision.HIGHEST
    blocks = N_BFLY
    devices = N_BFLY * N_CBLK
    tiled = source.reshape(devices, TILES, TILE, C)
    picked = jnp.take_along_axis(tiled, skeleton.astype(jnp.int32)[:, :, None, None], axis=1)
    picked = picked.reshape(blocks, ROWS_BLK, C).astype(jnp.float32)
    leaves = basis.reshape(blocks, ROWS_BLK, R).astype(jnp.float32)
    coefficient = jnp.einsum('bmr,bmc->brc', leaves, picked, precision=highest)
    factors = transfer.astype(jnp.float32)
    first = factors[:, :, :, :R]
    second = factors[:, :, :, R:]
    for level in range(LEVELS):
        partner = np.arange(blocks) ^ 1 << level
        coefficient = jnp.einsum('bij,bjc->bic', first[level], coefficient, precision=highest) + jnp.einsum('bij,bjc->bic', second[level], coefficient[partner], precision=highest)
    carried = coefficient.astype(jnp.bfloat16)
    factor_rho = math.sqrt(ROWS_BLK / R)
    mapped = factor_rho * jnp.einsum('bmr,brc->bmc', leaves, carried.astype(jnp.float32), precision=highest)
    mapped = mapped.reshape(ROWS, C)
    linear = linear_table[row_class]
    cubic = cubic_table[row_class]
    weighted = (mapped * (linear + cubic * mapped * mapped)).astype(jnp.bfloat16)
    weighted = weighted.reshape(blocks, ROWS_BLK, C).astype(jnp.float32)
    back = jnp.einsum('bmr,bmc->brc', leaves, weighted, precision=highest)
    for level in reversed(range(LEVELS)):
        partner = np.arange(blocks) ^ 1 << level
        sending = jnp.einsum('bji,bjc->bic', second[level], back, precision=highest)
        back = jnp.einsum('bji,bjc->bic', first[level], back, precision=highest) + sending[partner]
    returned = back.astype(jnp.bfloat16)
    ordered = (factor_rho * jnp.einsum('bmr,brc->bmc', leaves, returned.astype(jnp.float32), precision=highest)).astype(jnp.bfloat16)
    ordered = ordered.reshape(devices, TILES, TILE, C)
    inverse = jnp.argsort(skeleton, axis=1).astype(jnp.int32)
    adjoint = jnp.take_along_axis(ordered, inverse[:, :, None, None], axis=1)
    return adjoint.reshape(ROWS, C)
```

```python
import functools
import math

import jax
import jax.numpy as jnp
from jax import lax
from jax.experimental import pallas as pl
from jax.experimental.pallas import tpu as pltpu
from jax.sharding import PartitionSpec as P

MESH = pl.DeviceIdType.MESH
BF16, F32 = jnp.bfloat16, jnp.float32


def mm(left, right):
    return jnp.dot(left, right, preferred_element_type=F32)


def halves(value):
    high = value.astype(BF16)
    return high, (value - high.astype(F32)).astype(BF16)


def inverse_order(skeleton, tiles):
    order = [skeleton[0, i] for i in range(tiles)]
    inverse = []
    for j in range(tiles):
        place = jnp.int32(0)
        for i in range(1, tiles):
            place = jnp.where(order[i] == j, jnp.int32(i), place)
        inverse.append(place)
    return inverse


def core_kernel(
    n, levels, tiles, tile, rank, columns, rho,
    skeleton, classes, linear, cubic, source_any, basis_any, transfer_any,
    returned,
    source, basis, transfer, flipped, straight, turned, factors_t,
    lin, cub, weighted, whole,
    own32, part_out, part_in, level_out, level_in, share_out, share_in,
    local_sem, send_rs, recv_rs, send_lv, recv_lv, send_ag, recv_ag,
):
    share = columns // n
    rows = tiles * tile
    chunks = 4
    span = rows // chunks
    me = lax.axis_index("cblk")
    seat = lax.axis_index("bfly")

    def peer(k):
        return lax.rem(me + k, n)

    def partner(level):
        step = 1 << level
        return seat + (1 - 2 * lax.rem(seat // step, 2)) * step

    basis_copy = pltpu.make_async_copy(basis_any, basis, local_sem.at[0])
    basis_copy.start()
    source_copies = [
        pltpu.make_async_copy(
            source_any.at[pl.ds(c * span, span)], source.at[pl.ds(c * span, span)], local_sem.at[2 + c]
        )
        for c in range(chunks)
    ]
    for copy in source_copies:
        copy.start()
    transfer_copy = pltpu.make_async_copy(transfer_any, transfer, local_sem.at[1])
    transfer_copy.start()

    barrier = pltpu.get_barrier_semaphore()
    for k in range(1, n):
        pl.semaphore_signal(barrier, inc=1, device_id={"cblk": peer(k)}, device_id_type=MESH)
    for level in range(levels):
        pl.semaphore_signal(barrier, inc=1, device_id={"bfly": partner(level)}, device_id_type=MESH)

    inverse = inverse_order(skeleton, tiles)
    basis_copy.wait()
    for i in range(tiles):
        flipped[i] = basis[i].T
    for j in range(tiles):
        turned[:, j * tile:(j + 1) * tile] = flipped[inverse[j]]

    total = None
    for c in range(chunks):
        source_copies[c].wait()
        term = mm(turned[:, c * span:(c + 1) * span], source[c * span:(c + 1) * span, :])
        total = term if total is None else total + term

    def scatter(total, phase):
        for d in range(n):
            piece = total[:, d * share:(d + 1) * share]
            own32[d] = piece
            part_out[phase, d] = piece.astype(BF16)
        copies = []
        for k in range(1, n):
            copy = pltpu.make_async_remote_copy(
                src_ref=part_out.at[phase, peer(k)],
                dst_ref=part_in.at[phase, k - 1],
                send_sem=send_rs.at[phase, k - 1],
                recv_sem=recv_rs.at[phase, k - 1],
                device_id={"cblk": peer(k)},
                device_id_type=MESH,
            )
            copy.start()
            copies.append(copy)
        return copies

    def collect(copies, phase):
        value = own32[me]
        for k in range(1, n):
            copies[k - 1].wait()
            value = value + part_in[phase, k - 1].astype(F32)
        return value

    def exchange(phase, level):
        copy = pltpu.make_async_remote_copy(
            src_ref=level_out.at[phase, level],
            dst_ref=level_in.at[phase, level],
            send_sem=send_lv.at[phase, level],
            recv_sem=recv_lv.at[phase, level],
            device_id={"bfly": partner(level)},
            device_id_type=MESH,
        )
        copy.start()
        return copy

    def gather(value, phase):
        share_out[phase] = value.astype(BF16)
        share_in[phase, me] = value.astype(BF16)
        copies = []
        for k in range(1, n):
            copy = pltpu.make_async_remote_copy(
                src_ref=share_out.at[phase],
                dst_ref=share_in.at[phase, me],
                send_sem=send_ag.at[phase, k - 1],
                recv_sem=recv_ag.at[phase, k - 1],
                device_id={"cblk": peer(k)},
                device_id_type=MESH,
            )
            copy.start()
            copies.append(copy)
        return copies

    def assemble(copies, phase, target):
        for copy in copies:
            copy.wait()
        for d in range(n):
            target[:, d * share:(d + 1) * share] = share_in[phase, d]

    pl.semaphore_wait(barrier, n - 1 + levels)
    copies = scatter(total, 0)

    kinds = linear.shape[0]
    pieces = []
    for table in (linear[...], cubic[...]):
        high = table.astype(BF16)
        rest = table - high.astype(F32)
        middle = rest.astype(BF16)
        low = (rest - middle.astype(F32)).astype(BF16)
        pieces.append(jnp.concatenate([high, middle, low], axis=0))
    ids = lax.broadcasted_iota(jnp.int32, (kinds, tile), 0)
    for i in range(tiles):
        hot = jnp.where(classes[i:i + 1, :] == ids, F32(1), F32(0))
        hot = jnp.concatenate([hot, hot, hot], axis=0).T.astype(BF16)
        lin[i * tile:(i + 1) * tile, :] = mm(hot, pieces[0])
        cub[i * tile:(i + 1) * tile, :] = mm(hot, pieces[1])
        straight[:, i * tile:(i + 1) * tile] = flipped[i]
    transfer_copy.wait()
    for level in range(levels):
        factors_t[level] = transfer[level, 0].T

    value = collect(copies, 0)
    for level in range(levels):
        high, low = halves(value)
        level_out[0, level] = high
        copy = exchange(0, level)
        own = transfer[level, 0, :, :rank]
        value = mm(own, high) + mm(own, low)
        copy.wait()
        value = value + mm(transfer[level, 0, :, rank:], level_in[0, level])

    copies = gather(value, 0)
    assemble(copies, 0, whole)
    for c in range(chunks):
        at = slice(c * span, (c + 1) * span)
        left = basis[c * (tiles // chunks):(c + 1) * (tiles // chunks)].reshape(span, rank)
        mapped = rho * mm(left, whole[...])
        weighted[at, :] = (mapped * (lin[at, :] + cub[at, :] * mapped * mapped)).astype(BF16)
    back = mm(straight[...], weighted[...])

    copies = scatter(back, 1)
    value = collect(copies, 1)
    for level in reversed(range(levels)):
        high, low = halves(value)
        theirs = factors_t[level, rank:, :]
        level_out[1, level] = (mm(theirs, high) + mm(theirs, low)).astype(BF16)
        copy = exchange(1, level)
        own = factors_t[level, :rank, :]
        value = mm(own, high) + mm(own, low)
        copy.wait()
        value = value + level_in[1, level].astype(F32)
    copies = gather(value, 1)
    assemble(copies, 1, returned)


def expand_kernel(tiles, tile, rho, skeleton, basis, returned, out_any, ordered, sems):
    group = 2
    copies = []
    for g in range(tiles // group):
        left = basis[g * group * tile:(g + 1) * group * tile, :]
        value = (rho * mm(left, returned[...])).astype(BF16)
        for i in range(group):
            at = g * group + i
            ordered[at] = value[i * tile:(i + 1) * tile]
            copy = pltpu.make_async_copy(ordered.at[at], out_any.at[skeleton[0, at]], sems.at[at])
            copy.start()
            copies.append(copy)
    for copy in copies:
        copy.wait()


def per_device(source, basis, transfer, skeleton, row_class, linear_table, cubic_table):
    rows, columns = source.shape
    rank = basis.shape[1]
    tiles = skeleton.shape[1]
    tile = rows // tiles
    levels = transfer.shape[0]
    n = lax.axis_size("cblk")
    share = columns // n
    rho = math.sqrt(rows * n / rank)
    vmem = pl.BlockSpec(memory_space=pltpu.VMEM)
    smem = pl.BlockSpec(memory_space=pltpu.SMEM)
    anywhere = pl.BlockSpec(memory_space=pl.ANY)
    dma = pltpu.SemaphoreType.DMA
    returned = pl.pallas_call(
        functools.partial(core_kernel, n, levels, tiles, tile, rank, columns, rho),
        out_shape=jax.ShapeDtypeStruct((rank, columns), BF16),
        in_specs=[smem, vmem, vmem, vmem, anywhere, anywhere, anywhere],
        out_specs=vmem,
        scratch_shapes=[
            pltpu.VMEM((rows, columns), BF16),
            pltpu.VMEM((tiles, tile, rank), BF16),
            pltpu.VMEM(transfer.shape, BF16),
            pltpu.VMEM((tiles, rank, tile), BF16),
            pltpu.VMEM((rank, rows), BF16),
            pltpu.VMEM((rank, rows), BF16),
            pltpu.VMEM((levels, 2 * rank, rank), BF16),
            pltpu.VMEM((rows, columns), F32),
            pltpu.VMEM((rows, columns), F32),
            pltpu.VMEM((rows, columns), BF16),
            pltpu.VMEM((rank, columns), BF16),
            pltpu.VMEM((n, rank, share), F32),
            pltpu.VMEM((2, n, rank, share), BF16),
            pltpu.VMEM((2, n - 1, rank, share), BF16),
            pltpu.VMEM((2, levels, rank, share), BF16),
            pltpu.VMEM((2, levels, rank, share), BF16),
            pltpu.VMEM((2, rank, share), BF16),
            pltpu.VMEM((2, n, rank, share), BF16),
            dma((6,)),
            dma((2, n - 1)),
            dma((2, n - 1)),
            dma((2, levels)),
            dma((2, levels)),
            dma((2, n - 1)),
            dma((2, n - 1)),
        ],
        compiler_params=pltpu.CompilerParams(
            collective_id=0, has_side_effects=True, vmem_limit_bytes=48 << 20
        ),
        name="butterfly",
    )(
        skeleton,
        row_class.reshape(tiles, tile),
        linear_table,
        cubic_table,
        source,
        basis.reshape(tiles, tile, rank),
        transfer,
    )
    adjoint = pl.pallas_call(
        functools.partial(expand_kernel, tiles, tile, rho),
        out_shape=jax.ShapeDtypeStruct((tiles, tile, columns), BF16),
        in_specs=[smem, vmem, vmem],
        out_specs=anywhere,
        scratch_shapes=[pltpu.VMEM((tiles, tile, columns), BF16), dma((tiles,))],
        compiler_params=pltpu.CompilerParams(vmem_limit_bytes=24 << 20),
        name="expand",
    )(skeleton, basis, returned)
    return adjoint.reshape(rows, columns)


def solution(mesh):
    placed = (
        P(("ens", "bfly", "cblk"), None),
        P(("ens", "bfly", "cblk"), None),
        P("ens", "bfly", None, None),
        P(("ens", "bfly", "cblk"), None),
        P(("ens", "bfly", "cblk")),
        P(),
        P(),
    )
    return jax.shard_map(
        per_device,
        mesh=mesh,
        in_specs=placed,
        out_specs=P(("ens", "bfly", "cblk"), None),
        check_vma=False,
    )
```

```python
import functools
import math

import jax
import jax.numpy as jnp
from jax import lax
from jax.experimental import pallas as pl
from jax.experimental.pallas import tpu as pltpu
from jax.sharding import PartitionSpec as P

MESH = pl.DeviceIdType.MESH
BF16, F32 = jnp.bfloat16, jnp.float32
PARTS = 2


def mm(left, right):
    return jnp.dot(left, right, preferred_element_type=F32)


def halves(value):
    high = value.astype(BF16)
    return high, (value - high.astype(F32)).astype(BF16)


def inverse_order(skeleton, tiles):
    order = [skeleton[0, i] for i in range(tiles)]
    inverse = []
    for j in range(tiles):
        place = jnp.int32(0)
        for i in range(1, tiles):
            place = jnp.where(order[i] == j, jnp.int32(i), place)
        inverse.append(place)
    return inverse


def core_kernel(
    n, parts, levels, tiles, tile, rank, columns, rho,
    skeleton_any, classes_any, linear_any, cubic_any, source_any, basis_any, transfer_any,
    returned,
    skeleton, classes, linear, cubic,
    source, basis, transfer, flipped, straight, turned, factors_t,
    lin, cub, weighted,
    own32, part_out, part_in, level_out, level_in, share_out, share_in,
    small_sem, local_sem, send_rs, recv_rs, send_lv, recv_lv, send_ag, recv_ag,
):
    wide = columns // parts
    share = wide // n
    rows = tiles * tile
    me = lax.axis_index("cblk")
    seat = lax.axis_index("bfly")

    def peer(k):
        return lax.rem(me + k, n)

    def partner(level):
        step = 1 << level
        return seat + (1 - 2 * lax.rem(seat // step, 2)) * step

    smalls = [
        pltpu.make_async_copy(origin, target, small_sem.at[i])
        for i, (origin, target) in enumerate(
            [(skeleton_any, skeleton), (classes_any, classes), (linear_any, linear), (cubic_any, cubic)]
        )
    ]
    smalls[0].start()
    basis_copy = pltpu.make_async_copy(basis_any, basis, local_sem.at[0])
    basis_copy.start()
    source_copies = [
        pltpu.make_async_copy(
            source_any.at[:, pl.ds(h * wide, wide)], source.at[h], local_sem.at[2 + h]
        )
        for h in range(parts)
    ]
    for copy in source_copies:
        copy.start()
    transfer_copy = pltpu.make_async_copy(transfer_any, transfer, local_sem.at[1])
    transfer_copy.start()
    for copy in smalls[1:]:
        copy.start()

    barrier = pltpu.get_barrier_semaphore()
    for k in range(1, n):
        pl.semaphore_signal(barrier, inc=1, device_id={"cblk": peer(k)}, device_id_type=MESH)
    for level in range(levels):
        pl.semaphore_signal(barrier, inc=1, device_id={"bfly": partner(level)}, device_id_type=MESH)

    smalls[0].wait()
    inverse = inverse_order(skeleton, tiles)
    basis_copy.wait()
    for i in range(tiles):
        flipped[i] = basis[i].T
    for j in range(tiles):
        turned[:, j * tile:(j + 1) * tile] = flipped[inverse[j]]

    def scatter(total, phase, h):
        total = total.T
        copies = []
        for d in range(n):
            piece = total[d * share:(d + 1) * share]
            own32[phase, h, d] = piece
            part_out[phase, h, d] = piece.astype(BF16)
        for k in range(1, n):
            copy = pltpu.make_async_remote_copy(
                src_ref=part_out.at[phase, h, peer(k)],
                dst_ref=part_in.at[phase, h, k - 1],
                send_sem=send_rs.at[phase, h, k - 1],
                recv_sem=recv_rs.at[phase, h, k - 1],
                device_id={"cblk": peer(k)},
                device_id_type=MESH,
            )
            copy.start()
            copies.append(copy)
        return copies

    def collect(copies, phase, h):
        value = own32[phase, h, me]
        for k in range(1, n):
            copies[k - 1].wait_recv()
            value = value + part_in[phase, h, k - 1].astype(F32)
        sent.extend(copies)
        return value

    def exchange(phase, level, h):
        copy = pltpu.make_async_remote_copy(
            src_ref=level_out.at[phase, level, h],
            dst_ref=level_in.at[phase, level, h],
            send_sem=send_lv.at[phase, level, h],
            recv_sem=recv_lv.at[phase, level, h],
            device_id={"bfly": partner(level)},
            device_id_type=MESH,
        )
        copy.start()
        return copy

    def gather(value, phase, h):
        share_out[phase, h] = value.astype(BF16)
        copies = []
        for k in range(1, n):
            copy = pltpu.make_async_remote_copy(
                src_ref=share_out.at[phase, h],
                dst_ref=share_in.at[phase, h, me],
                send_sem=send_ag.at[phase, h, k - 1],
                recv_sem=recv_ag.at[phase, h, k - 1],
                device_id={"cblk": peer(k)},
                device_id_type=MESH,
            )
            copy.start()
            copies.append(copy)
        share_in[phase, h, me] = value.astype(BF16)
        return copies

    def arrive(copies):
        for copy in copies:
            copy.wait_recv()
        sent.extend(copies)

    def doubled(value, factor):
        high, low = halves(value)
        both = mm(jnp.concatenate([high, low], axis=0), factor)
        return both[:share] + both[share:]

    sent = []
    halves_range = range(parts)
    scattered = []
    for h in halves_range:
        source_copies[h].wait()
        total = mm(turned[...], source[h])
        if h == 0:
            pl.semaphore_wait(barrier, n - 1 + levels)
        scattered.append(scatter(total, 0, h))

    transfer_copy.wait()
    for level in range(levels):
        factors_t[level] = transfer[level, 0].T
    for copy in smalls[1:]:
        copy.wait()
    kinds = linear.shape[0]
    pieces = []
    for table in (linear[...], cubic[...]):
        high = table.astype(BF16)
        rest = table - high.astype(F32)
        middle = rest.astype(BF16)
        low = (rest - middle.astype(F32)).astype(BF16)
        pieces.append(jnp.concatenate([high, middle, low], axis=0))
    ids = lax.broadcasted_iota(jnp.int32, (kinds, tile), 0)
    for i in range(tiles):
        hot = jnp.where(classes[i:i + 1, :] == ids, F32(1), F32(0))
        hot = jnp.concatenate([hot, hot, hot], axis=0).T.astype(BF16)
        lin[i * tile:(i + 1) * tile, :] = mm(hot, pieces[0])
        cub[i * tile:(i + 1) * tile, :] = mm(hot, pieces[1])
        straight[:, i * tile:(i + 1) * tile] = flipped[i]

    values = [None] * parts
    for level in range(levels):
        copies = []
        for h in halves_range:
            if level == 0:
                values[h] = collect(scattered[h], 0, h)
            level_out[0, level, h] = values[h].astype(BF16)
            copies.append(exchange(0, level, h))
            values[h] = doubled(values[h], factors_t[level, :rank, :])
        for h in halves_range:
            copies[h].wait_recv()
            values[h] = values[h] + mm(level_in[0, level, h], factors_t[level, rank:, :])
            sent.append(copies[h])
    copies = [gather(values[h], 0, h) for h in halves_range]

    scattered = []
    for h in halves_range:
        arrive(copies[h])
        whole = share_in[0, h].reshape(wide, rank)
        at = slice(h * wide, (h + 1) * wide)
        chunks = 4
        span = rows // chunks
        for c in range(chunks):
            down = slice(c * span, (c + 1) * span)
            left = basis[c * (tiles // chunks):(c + 1) * (tiles // chunks)].reshape(span, rank)
            mapped = rho * lax.dot_general(
                left, whole, (((1,), (1,)), ((), ())), preferred_element_type=F32
            )
            weighted[h, down, :] = (
                mapped * (lin[down, at] + cub[down, at] * mapped * mapped)
            ).astype(BF16)
        scattered.append(scatter(mm(straight[...], weighted[h]), 1, h))

    for level in reversed(range(levels)):
        copies = []
        for h in halves_range:
            if level == levels - 1:
                values[h] = collect(scattered[h], 1, h)
            level_out[1, level, h] = doubled(values[h], transfer[level, 0, :, rank:]).astype(BF16)
            copies.append(exchange(1, level, h))
            values[h] = doubled(values[h], transfer[level, 0, :, :rank])
        for h in halves_range:
            copies[h].wait_recv()
            values[h] = values[h] + level_in[1, level, h].astype(F32)
            sent.append(copies[h])
    copies = [gather(values[h], 1, h) for h in halves_range]
    for h in halves_range:
        arrive(copies[h])
        returned[h] = share_in[1, h]
    for copy in sent:
        copy.wait_send()


def expand_kernel(
    tiles, tile, rho, skeleton_any, basis_any, returned_any, out_any,
    skeleton, basis, returned, ordered, load_sems, sems,
):
    group = 2
    loads = [
        pltpu.make_async_copy(origin, target, load_sems.at[i])
        for i, (origin, target) in enumerate(
            [(returned_any, returned), (basis_any, basis), (skeleton_any, skeleton)]
        )
    ]
    for copy in loads:
        copy.start()
    for copy in loads:
        copy.wait()
    copies = []
    for g in range(tiles // group):
        left = basis[g * group * tile:(g + 1) * group * tile, :]
        value = rho * lax.dot_general(
            left, returned[...], (((1,), (1,)), ((), ())), preferred_element_type=F32
        )
        value = value.astype(BF16)
        for i in range(group):
            at = g * group + i
            ordered[at] = value[i * tile:(i + 1) * tile]
            copy = pltpu.make_async_copy(ordered.at[at], out_any.at[skeleton[0, at]], sems.at[at])
            copy.start()
            copies.append(copy)
    for copy in copies:
        copy.wait()


def per_device(source, basis, transfer, skeleton, row_class, linear_table, cubic_table):
    rows, columns = source.shape
    rank = basis.shape[1]
    tiles = skeleton.shape[1]
    tile = rows // tiles
    levels = transfer.shape[0]
    n = lax.axis_size("cblk")
    parts = PARTS
    wide = columns // parts
    share = wide // n
    rho = math.sqrt(rows * n / rank)
    vmem = pl.BlockSpec(memory_space=pltpu.VMEM)
    anywhere = pl.BlockSpec(memory_space=pl.ANY)
    dma = pltpu.SemaphoreType.DMA
    returned = pl.pallas_call(
        functools.partial(core_kernel, n, parts, levels, tiles, tile, rank, columns, rho),
        out_shape=jax.ShapeDtypeStruct((parts, n, share, rank), BF16),
        in_specs=[anywhere] * 7,
        out_specs=vmem,
        scratch_shapes=[
            pltpu.SMEM(skeleton.shape, jnp.int32),
            pltpu.VMEM((tiles, tile), jnp.int32),
            pltpu.VMEM(linear_table.shape, F32),
            pltpu.VMEM(cubic_table.shape, F32),
            pltpu.VMEM((parts, rows, wide), BF16),
            pltpu.VMEM((tiles, tile, rank), BF16),
            pltpu.VMEM(transfer.shape, BF16),
            pltpu.VMEM((tiles, rank, tile), BF16),
            pltpu.VMEM((rank, rows), BF16),
            pltpu.VMEM((rank, rows), BF16),
            pltpu.VMEM((levels, 2 * rank, rank), BF16),
            pltpu.VMEM((rows, columns), F32),
            pltpu.VMEM((rows, columns), F32),
            pltpu.VMEM((parts, rows, wide), BF16),
            pltpu.VMEM((2, parts, n, share, rank), F32),
            pltpu.VMEM((2, parts, n, share, rank), BF16),
            pltpu.VMEM((2, parts, n - 1, share, rank), BF16),
            pltpu.VMEM((2, levels, parts, share, rank), BF16),
            pltpu.VMEM((2, levels, parts, share, rank), BF16),
            pltpu.VMEM((2, parts, share, rank), BF16),
            pltpu.VMEM((2, parts, n, share, rank), BF16),
            dma((4,)),
            dma((2 + parts,)),
            dma((2, parts, n - 1)),
            dma((2, parts, n - 1)),
            dma((2, levels, parts)),
            dma((2, levels, parts)),
            dma((2, parts, n - 1)),
            dma((2, parts, n - 1)),
        ],
        compiler_params=pltpu.CompilerParams(
            collective_id=0, has_side_effects=True, vmem_limit_bytes=67043328
        ),
        name="butterfly",
    )(
        skeleton,
        row_class.reshape(tiles, tile),
        linear_table,
        cubic_table,
        source,
        basis.reshape(tiles, tile, rank),
        transfer,
    )
    adjoint = pl.pallas_call(
        functools.partial(expand_kernel, tiles, tile, rho),
        out_shape=jax.ShapeDtypeStruct((tiles, tile, columns), BF16),
        in_specs=[anywhere] * 3,
        out_specs=anywhere,
        scratch_shapes=[
            pltpu.SMEM(skeleton.shape, jnp.int32),
            pltpu.VMEM(basis.shape, BF16),
            pltpu.VMEM((columns, rank), BF16),
            pltpu.VMEM((tiles, tile, columns), BF16),
            dma((3,)),
            dma((tiles,)),
        ],
        compiler_params=pltpu.CompilerParams(vmem_limit_bytes=67043328),
        name="expand",
    )(skeleton, basis, returned.reshape(columns, rank))
    return adjoint.reshape(rows, columns)


def solution(mesh):
    placed = (
        P(("ens", "bfly", "cblk"), None),
        P(("ens", "bfly", "cblk"), None),
        P("ens", "bfly", None, None),
        P(("ens", "bfly", "cblk"), None),
        P(("ens", "bfly", "cblk")),
        P(),
        P(),
    )
    return jax.shard_map(
        per_device,
        mesh=mesh,
        in_specs=placed,
        out_specs=P(("ens", "bfly", "cblk"), None),
        check_vma=False,
    )
```

```python
import functools
import math

import jax
import jax.numpy as jnp
from jax import lax
from jax.experimental import pallas as pl
from jax.experimental.pallas import tpu as pltpu
from jax.sharding import PartitionSpec as P

MESH = pl.DeviceIdType.MESH
BF16, F32 = jnp.bfloat16, jnp.float32
PARTS = 2


def mm(left, right):
    return jnp.dot(left, right, preferred_element_type=F32)


def halves(value):
    high = value.astype(BF16)
    return high, (value - high.astype(F32)).astype(BF16)


def inverse_order(skeleton, tiles):
    order = [skeleton[0, i] for i in range(tiles)]
    inverse = []
    for j in range(tiles):
        place = jnp.int32(0)
        for i in range(1, tiles):
            place = jnp.where(order[i] == j, jnp.int32(i), place)
        inverse.append(place)
    return inverse


def core_kernel(
    n, parts, levels, tiles, tile, rank, columns, rho,
    skeleton_any, classes_any, linear_any, cubic_any, source_any, basis_any, transfer_any,
    returned,
    skeleton, classes, linear, cubic,
    source, basis, transfer, flipped, straight, turned, factors_t,
    lin, cub, weighted,
    own32, part_out, part_in, level_out, level_in, share_out, share_in,
    small_sem, keep_sem, local_sem, send_rs, recv_rs, send_lv, recv_lv, send_ag, recv_ag,
):
    wide = columns // parts
    share = wide // n
    rows = tiles * tile
    me = lax.axis_index("cblk")
    seat = lax.axis_index("bfly")

    def peer(k):
        return lax.rem(me + k, n)

    def partner(level):
        step = 1 << level
        return seat + (1 - 2 * lax.rem(seat // step, 2)) * step

    barrier = pltpu.get_barrier_semaphore()
    for k in range(1, n):
        pl.semaphore_signal(barrier, inc=1, device_id={"cblk": peer(k)}, device_id_type=MESH)
    for level in range(levels):
        pl.semaphore_signal(barrier, inc=1, device_id={"bfly": partner(level)}, device_id_type=MESH)

    smalls = [
        pltpu.make_async_copy(origin, target, small_sem.at[i])
        for i, (origin, target) in enumerate(
            [(skeleton_any, skeleton), (classes_any, classes), (linear_any, linear), (cubic_any, cubic)]
        )
    ]
    smalls[0].start()
    basis_copy = pltpu.make_async_copy(basis_any, basis, local_sem.at[0])
    basis_copy.start()
    source_copies = [
        pltpu.make_async_copy(
            source_any.at[:, pl.ds(h * wide, wide)], source.at[h], local_sem.at[2 + h]
        )
        for h in range(parts)
    ]
    for copy in source_copies:
        copy.start()
    transfer_copy = pltpu.make_async_copy(transfer_any, transfer, local_sem.at[1])
    transfer_copy.start()
    for copy in smalls[1:]:
        copy.start()

    smalls[0].wait()
    inverse = inverse_order(skeleton, tiles)
    basis_copy.wait()
    for i in range(tiles):
        flipped[i] = basis[i].T
    for j in range(tiles):
        turned[:, j * tile:(j + 1) * tile] = flipped[inverse[j]]

    def scatter(total, phase, h):
        total = total.T
        copies = []
        for d in range(n):
            piece = total[d * share:(d + 1) * share]
            own32[phase, h, d] = piece
            part_out[phase, h, d] = piece.astype(BF16)
        for k in range(1, n):
            copy = pltpu.make_async_remote_copy(
                src_ref=part_out.at[phase, h, peer(k)],
                dst_ref=part_in.at[phase, h, k - 1],
                send_sem=send_rs.at[phase, h, k - 1],
                recv_sem=recv_rs.at[phase, h, k - 1],
                device_id={"cblk": peer(k)},
                device_id_type=MESH,
            )
            copy.start()
            copies.append(copy)
        return copies

    def collect(copies, phase, h):
        value = own32[phase, h, me]
        for k in range(1, n):
            copies[k - 1].wait_recv()
            value = value + part_in[phase, h, k - 1].astype(F32)
        sent.extend(copies)
        return value

    def exchange(phase, level, h):
        copy = pltpu.make_async_remote_copy(
            src_ref=level_out.at[phase, level, h],
            dst_ref=level_in.at[phase, level, h],
            send_sem=send_lv.at[phase, level, h],
            recv_sem=recv_lv.at[phase, level, h],
            device_id={"bfly": partner(level)},
            device_id_type=MESH,
        )
        copy.start()
        return copy

    def landing(phase):
        return share_in if phase == 0 else returned

    def gather(value, phase, h):
        share_out[phase, h] = value.astype(BF16)
        copies = []
        for k in range(1, n):
            copy = pltpu.make_async_remote_copy(
                src_ref=share_out.at[phase, h],
                dst_ref=landing(phase).at[h, me],
                send_sem=send_ag.at[phase, h, k - 1],
                recv_sem=recv_ag.at[phase, h, k - 1],
                device_id={"cblk": peer(k)},
                device_id_type=MESH,
            )
            copy.start()
            copies.append(copy)
        if phase == 0:
            share_in[h, me] = value.astype(BF16)
        else:
            keep = pltpu.make_async_copy(share_out.at[1, h], returned.at[h, me], keep_sem.at[h])
            keep.start()
            keeps.append(keep)
        return copies

    def arrive(copies):
        for copy in copies:
            copy.wait_recv()
        sent.extend(copies)

    def doubled(value, factor):
        high, low = halves(value)
        both = mm(jnp.concatenate([high, low], axis=0), factor)
        return both[:share] + both[share:]

    sent = []
    keeps = []
    halves_range = range(parts)
    scattered = []
    for h in halves_range:
        source_copies[h].wait()
        total = mm(turned[...], source[h])
        if h == 0:
            pl.semaphore_wait(barrier, n - 1 + levels)
        scattered.append(scatter(total, 0, h))

    transfer_copy.wait()
    for level in range(levels):
        factors_t[level] = transfer[level, 0].T
    for copy in smalls[1:]:
        copy.wait()
    kinds = linear.shape[0]
    pieces = []
    for table in (linear[...], cubic[...]):
        high = table.astype(BF16)
        rest = table - high.astype(F32)
        middle = rest.astype(BF16)
        low = (rest - middle.astype(F32)).astype(BF16)
        pieces.append(jnp.concatenate([high, middle, low], axis=0))
    ids = lax.broadcasted_iota(jnp.int32, (kinds, tile), 0)
    for i in range(tiles):
        hot = jnp.where(classes[i:i + 1, :] == ids, F32(1), F32(0))
        hot = jnp.concatenate([hot, hot, hot], axis=0).T.astype(BF16)
        lin[i * tile:(i + 1) * tile, :] = mm(hot, pieces[0])
        cub[i * tile:(i + 1) * tile, :] = mm(hot, pieces[1])
        straight[:, i * tile:(i + 1) * tile] = flipped[i]

    values = [None] * parts
    for level in range(levels):
        copies = []
        for h in halves_range:
            if level == 0:
                values[h] = collect(scattered[h], 0, h)
            level_out[0, level, h] = values[h].astype(BF16)
            copies.append(exchange(0, level, h))
            values[h] = doubled(values[h], factors_t[level, :rank, :])
        for h in halves_range:
            copies[h].wait_recv()
            values[h] = values[h] + mm(level_in[0, level, h], factors_t[level, rank:, :])
            sent.append(copies[h])
    copies = [gather(values[h], 0, h) for h in halves_range]

    scattered = []
    for h in halves_range:
        arrive(copies[h])
        whole = share_in[h].reshape(wide, rank).T
        at = slice(h * wide, (h + 1) * wide)
        chunks = 4
        span = rows // chunks
        for c in range(chunks):
            down = slice(c * span, (c + 1) * span)
            left = basis[c * (tiles // chunks):(c + 1) * (tiles // chunks)].reshape(span, rank)
            mapped = rho * mm(left, whole)
            weighted[h, down, :] = (
                mapped * (lin[down, at] + cub[down, at] * mapped * mapped)
            ).astype(BF16)
        scattered.append(scatter(mm(straight[...], weighted[h]), 1, h))

    for level in reversed(range(levels)):
        copies = []
        for h in halves_range:
            if level == levels - 1:
                values[h] = collect(scattered[h], 1, h)
            level_out[1, level, h] = doubled(values[h], transfer[level, 0, :, rank:]).astype(BF16)
            copies.append(exchange(1, level, h))
            values[h] = doubled(values[h], transfer[level, 0, :, :rank])
        for h in halves_range:
            copies[h].wait_recv()
            values[h] = values[h] + level_in[1, level, h].astype(F32)
            sent.append(copies[h])
    copies = [gather(values[h], 1, h) for h in halves_range]
    for h in halves_range:
        arrive(copies[h])
        keeps[h].wait()
    for copy in sent:
        copy.wait_send()


def expand_kernel(
    tiles, tile, rho, skeleton_any, basis_any, returned_any, out_any,
    skeleton, basis, returned, ordered, load_sems, sems,
):
    group = 4
    span = group * tile
    loads = [
        pltpu.make_async_copy(origin, target, load_sems.at[i])
        for i, (origin, target) in enumerate([(returned_any, returned), (skeleton_any, skeleton)])
    ]
    loads += [
        pltpu.make_async_copy(
            basis_any.at[pl.ds(g * span, span)], basis.at[pl.ds(g * span, span)], load_sems.at[2 + g]
        )
        for g in range(tiles // group)
    ]
    for copy in loads:
        copy.start()
    loads[0].wait()
    right = returned[...].T
    loads[1].wait()
    copies = []
    for g in range(tiles // group):
        loads[2 + g].wait()
        value = (rho * mm(basis[g * span:(g + 1) * span, :], right)).astype(BF16)
        for i in range(group):
            at = g * group + i
            ordered[at] = value[i * tile:(i + 1) * tile]
            copy = pltpu.make_async_copy(ordered.at[at], out_any.at[skeleton[0, at]], sems.at[at])
            copy.start()
            copies.append(copy)
    for copy in copies:
        copy.wait()


def per_device(source, basis, transfer, skeleton, row_class, linear_table, cubic_table):
    rows, columns = source.shape
    rank = basis.shape[1]
    tiles = skeleton.shape[1]
    tile = rows // tiles
    levels = transfer.shape[0]
    n = lax.axis_size("cblk")
    parts = PARTS
    wide = columns // parts
    share = wide // n
    rho = math.sqrt(rows * n / rank)
    anywhere = pl.BlockSpec(memory_space=pl.ANY)
    dma = pltpu.SemaphoreType.DMA
    returned = pl.pallas_call(
        functools.partial(core_kernel, n, parts, levels, tiles, tile, rank, columns, rho),
        out_shape=jax.ShapeDtypeStruct((parts, n, share, rank), BF16),
        in_specs=[anywhere] * 7,
        out_specs=anywhere,
        scratch_shapes=[
            pltpu.SMEM(skeleton.shape, jnp.int32),
            pltpu.VMEM((tiles, tile), jnp.int32),
            pltpu.VMEM(linear_table.shape, F32),
            pltpu.VMEM(cubic_table.shape, F32),
            pltpu.VMEM((parts, rows, wide), BF16),
            pltpu.VMEM((tiles, tile, rank), BF16),
            pltpu.VMEM(transfer.shape, BF16),
            pltpu.VMEM((tiles, rank, tile), BF16),
            pltpu.VMEM((rank, rows), BF16),
            pltpu.VMEM((rank, rows), BF16),
            pltpu.VMEM((levels, 2 * rank, rank), BF16),
            pltpu.VMEM((rows, columns), F32),
            pltpu.VMEM((rows, columns), F32),
            pltpu.VMEM((parts, rows, wide), BF16),
            pltpu.VMEM((2, parts, n, share, rank), F32),
            pltpu.VMEM((2, parts, n, share, rank), BF16),
            pltpu.VMEM((2, parts, n - 1, share, rank), BF16),
            pltpu.VMEM((2, levels, parts, share, rank), BF16),
            pltpu.VMEM((2, levels, parts, share, rank), BF16),
            pltpu.VMEM((2, parts, share, rank), BF16),
            pltpu.VMEM((parts, n, share, rank), BF16),
            dma((4,)),
            dma((parts,)),
            dma((2 + parts,)),
            dma((2, parts, n - 1)),
            dma((2, parts, n - 1)),
            dma((2, levels, parts)),
            dma((2, levels, parts)),
            dma((2, parts, n - 1)),
            dma((2, parts, n - 1)),
        ],
        compiler_params=pltpu.CompilerParams(
            collective_id=0, has_side_effects=True, vmem_limit_bytes=67043328
        ),
        name="butterfly",
    )(
        skeleton,
        row_class.reshape(tiles, tile),
        linear_table,
        cubic_table,
        source,
        basis.reshape(tiles, tile, rank),
        transfer,
    )
    adjoint = pl.pallas_call(
        functools.partial(expand_kernel, tiles, tile, rho),
        out_shape=jax.ShapeDtypeStruct((tiles, tile, columns), BF16),
        in_specs=[anywhere] * 3,
        out_specs=anywhere,
        scratch_shapes=[
            pltpu.SMEM(skeleton.shape, jnp.int32),
            pltpu.VMEM(basis.shape, BF16),
            pltpu.VMEM((columns, rank), BF16),
            pltpu.VMEM((tiles, tile, columns), BF16),
            dma((2 + tiles // 4,)),
            dma((tiles,)),
        ],
        compiler_params=pltpu.CompilerParams(vmem_limit_bytes=67043328),
        name="expand",
    )(skeleton, basis, returned.reshape(columns, rank))
    return adjoint.reshape(rows, columns)


def solution(mesh):
    placed = (
        P(("ens", "bfly", "cblk"), None),
        P(("ens", "bfly", "cblk"), None),
        P("ens", "bfly", None, None),
        P(("ens", "bfly", "cblk"), None),
        P(("ens", "bfly", "cblk")),
        P(),
        P(),
    )
    return jax.shard_map(
        per_device,
        mesh=mesh,
        in_specs=placed,
        out_specs=P(("ens", "bfly", "cblk"), None),
        check_vma=False,
    )
```

```python
import functools
import math

import jax
import jax.numpy as jnp
from jax import lax
from jax.experimental import pallas as pl
from jax.experimental.pallas import tpu as pltpu
from jax.sharding import PartitionSpec as P

MESH = pl.DeviceIdType.MESH
BF16, F32 = jnp.bfloat16, jnp.float32
PARTS = 2


def mm(left, right):
    return jnp.dot(left, right, preferred_element_type=F32)


def halves(value):
    high = value.astype(BF16)
    return high, (value - high.astype(F32)).astype(BF16)


def inverse_order(skeleton, tiles):
    order = [skeleton[0, i] for i in range(tiles)]
    inverse = []
    for j in range(tiles):
        place = jnp.int32(0)
        for i in range(1, tiles):
            place = jnp.where(order[i] == j, jnp.int32(i), place)
        inverse.append(place)
    return inverse


def core_kernel(
    n, parts, levels, tiles, tile, rank, columns, rho,
    skeleton_any, classes_any, linear_any, cubic_any, source_any, basis_any, transfer_any,
    returned,
    skeleton, classes, linear, cubic,
    source, basis, transfer, flipped, straight, turned, factors_t,
    lin, cub, weighted,
    own32, part_out, part_in, level_out, level_in, share_out, share_in,
    small_sem, keep_sem, local_sem, send_rs, recv_rs, send_lv, recv_lv, send_ag, recv_ag,
):
    wide = columns // parts
    share = wide // n
    rows = tiles * tile
    me = lax.axis_index("cblk")
    seat = lax.axis_index("bfly")

    def peer(k):
        return lax.rem(me + k, n)

    def partner(level):
        step = 1 << level
        return seat + (1 - 2 * lax.rem(seat // step, 2)) * step

    barrier = pltpu.get_barrier_semaphore()
    for k in range(1, n):
        pl.semaphore_signal(barrier, inc=1, device_id={"cblk": peer(k)}, device_id_type=MESH)
    for level in range(levels):
        pl.semaphore_signal(barrier, inc=1, device_id={"bfly": partner(level)}, device_id_type=MESH)

    smalls = [
        pltpu.make_async_copy(origin, target, small_sem.at[i])
        for i, (origin, target) in enumerate(
            [(skeleton_any, skeleton), (classes_any, classes), (linear_any, linear), (cubic_any, cubic)]
        )
    ]
    smalls[0].start()
    basis_copy = pltpu.make_async_copy(basis_any, basis, local_sem.at[0])
    basis_copy.start()
    source_copies = [
        pltpu.make_async_copy(
            source_any.at[:, pl.ds(h * wide, wide)], source.at[h], local_sem.at[2 + h]
        )
        for h in range(parts)
    ]
    for copy in source_copies:
        copy.start()
    transfer_copy = pltpu.make_async_copy(transfer_any, transfer, local_sem.at[1])
    transfer_copy.start()
    for copy in smalls[1:]:
        copy.start()

    smalls[0].wait()
    inverse = inverse_order(skeleton, tiles)
    basis_copy.wait()
    for i in range(tiles):
        flipped[i] = basis[i].T
    for j in range(tiles):
        turned[:, j * tile:(j + 1) * tile] = flipped[inverse[j]]

    def scatter(total, phase, h):
        total = total.T
        copies = []
        for d in range(n):
            piece = total[d * share:(d + 1) * share]
            own32[phase, h, d] = piece
            part_out[phase, h, d] = piece.astype(BF16)
        for k in range(1, n):
            copy = pltpu.make_async_remote_copy(
                src_ref=part_out.at[phase, h, peer(k)],
                dst_ref=part_in.at[phase, h, k - 1],
                send_sem=send_rs.at[phase, h, k - 1],
                recv_sem=recv_rs.at[phase, h, k - 1],
                device_id={"cblk": peer(k)},
                device_id_type=MESH,
            )
            copy.start()
            copies.append(copy)
        return copies

    def collect(copies, phase, h):
        value = own32[phase, h, me]
        for k in range(1, n):
            copies[k - 1].wait_recv()
            value = value + part_in[phase, h, k - 1].astype(F32)
        sent.extend(copies)
        return value

    def exchange(phase, level, h):
        copy = pltpu.make_async_remote_copy(
            src_ref=level_out.at[phase, level, h],
            dst_ref=level_in.at[phase, level, h],
            send_sem=send_lv.at[phase, level, h],
            recv_sem=recv_lv.at[phase, level, h],
            device_id={"bfly": partner(level)},
            device_id_type=MESH,
        )
        copy.start()
        return copy

    def landing(phase):
        return share_in if phase == 0 else returned

    def gather(value, phase, h):
        share_out[phase, h] = value.astype(BF16)
        copies = []
        for k in range(1, n):
            copy = pltpu.make_async_remote_copy(
                src_ref=share_out.at[phase, h],
                dst_ref=landing(phase).at[h, me],
                send_sem=send_ag.at[phase, h, k - 1],
                recv_sem=recv_ag.at[phase, h, k - 1],
                device_id={"cblk": peer(k)},
                device_id_type=MESH,
            )
            copy.start()
            copies.append(copy)
        if phase == 0:
            share_in[h, me] = value.astype(BF16)
        else:
            keep = pltpu.make_async_copy(share_out.at[1, h], returned.at[h, me], keep_sem.at[h])
            keep.start()
            keeps.append(keep)
        return copies

    def arrive(copies):
        for copy in copies:
            copy.wait_recv()
        sent.extend(copies)

    def doubled(value, factor):
        high, low = halves(value)
        both = mm(jnp.concatenate([high, low], axis=0), factor)
        return both[:share] + both[share:]

    sent = []
    keeps = []
    halves_range = range(parts)
    scattered = []
    for h in halves_range:
        source_copies[h].wait()
        total = mm(turned[...], source[h])
        if h == 0:
            pl.semaphore_wait(barrier, n - 1 + levels)
        scattered.append(scatter(total, 0, h))

    transfer_copy.wait()
    for level in range(levels):
        factors_t[level] = transfer[level, 0].T
    for copy in smalls[1:]:
        copy.wait()
    kinds = linear.shape[0]
    pieces = []
    for table in (linear[...], cubic[...]):
        high = table.astype(BF16)
        rest = table - high.astype(F32)
        middle = rest.astype(BF16)
        low = (rest - middle.astype(F32)).astype(BF16)
        pieces.append(jnp.concatenate([high, middle, low], axis=0))
    ids = lax.broadcasted_iota(jnp.int32, (kinds, tile), 0)
    for i in range(tiles):
        hot = jnp.where(classes[i:i + 1, :] == ids, F32(1), F32(0))
        hot = jnp.concatenate([hot, hot, hot], axis=0).T.astype(BF16)
        lin[i * tile:(i + 1) * tile, :] = mm(hot, pieces[0])
        cub[i * tile:(i + 1) * tile, :] = mm(hot, pieces[1])
        straight[:, i * tile:(i + 1) * tile] = flipped[i]

    values = [None] * parts
    for level in range(levels):
        copies = []
        for h in halves_range:
            if level == 0:
                values[h] = collect(scattered[h], 0, h)
            level_out[0, level, h] = values[h].astype(BF16)
            copies.append(exchange(0, level, h))
            values[h] = doubled(values[h], factors_t[level, :rank, :])
        for h in halves_range:
            copies[h].wait_recv()
            values[h] = values[h] + mm(level_in[0, level, h], factors_t[level, rank:, :])
            sent.append(copies[h])
    copies = [gather(values[h], 0, h) for h in halves_range]

    scattered = []
    for h in halves_range:
        arrive(copies[h])
        whole = share_in[h].reshape(wide, rank).T
        at = slice(h * wide, (h + 1) * wide)
        chunks = 4
        span = rows // chunks
        for c in range(chunks):
            down = slice(c * span, (c + 1) * span)
            left = basis[c * (tiles // chunks):(c + 1) * (tiles // chunks)].reshape(span, rank)
            mapped = rho * mm(left, whole)
            weighted[h, down, :] = (
                mapped * (lin[down, at] + cub[down, at] * mapped * mapped)
            ).astype(BF16)
        scattered.append(scatter(mm(straight[...], weighted[h]), 1, h))

    for level in reversed(range(levels)):
        copies = []
        for h in halves_range:
            if level == levels - 1:
                values[h] = collect(scattered[h], 1, h)
            level_out[1, level, h] = doubled(values[h], transfer[level, 0, :, rank:]).astype(BF16)
            copies.append(exchange(1, level, h))
            values[h] = doubled(values[h], transfer[level, 0, :, :rank])
        for h in halves_range:
            copies[h].wait_recv()
            values[h] = values[h] + level_in[1, level, h].astype(F32)
            sent.append(copies[h])
    copies = [gather(values[h], 1, h) for h in halves_range]
    for h in halves_range:
        arrive(copies[h])
        keeps[h].wait()
    for copy in sent:
        copy.wait_send()


def expand_kernel(
    tiles, tile, rho, skeleton_any, basis_any, returned_any, out_any,
    skeleton, basis, returned, ordered, load_sems, sems,
):
    group = 4
    span = group * tile
    loads = [
        pltpu.make_async_copy(origin, target, load_sems.at[i])
        for i, (origin, target) in enumerate([(returned_any, returned), (skeleton_any, skeleton)])
    ]
    loads.append(pltpu.make_async_copy(basis_any, basis, load_sems.at[2]))
    for copy in loads:
        copy.start()
    loads[0].wait()
    loads[1].wait()
    copies = []
    for g in range(tiles // group):
        if g == 0:
            loads[2].wait()
        value = (rho * lax.dot_general(basis[g * span:(g + 1) * span, :], returned[...], (((1,), (1,)), ((), ())), preferred_element_type=F32)).astype(BF16)
        for i in range(group):
            at = g * group + i
            ordered[at] = value[i * tile:(i + 1) * tile]
            copy = pltpu.make_async_copy(ordered.at[at], out_any.at[skeleton[0, at]], sems.at[at])
            copy.start()
            copies.append(copy)
    for copy in copies:
        copy.wait()


def per_device(source, basis, transfer, skeleton, row_class, linear_table, cubic_table):
    rows, columns = source.shape
    rank = basis.shape[1]
    tiles = skeleton.shape[1]
    tile = rows // tiles
    levels = transfer.shape[0]
    n = lax.axis_size("cblk")
    parts = PARTS
    wide = columns // parts
    share = wide // n
    rho = math.sqrt(rows * n / rank)
    anywhere = pl.BlockSpec(memory_space=pl.ANY)
    dma = pltpu.SemaphoreType.DMA
    returned = pl.pallas_call(
        functools.partial(core_kernel, n, parts, levels, tiles, tile, rank, columns, rho),
        out_shape=jax.ShapeDtypeStruct((parts, n, share, rank), BF16),
        in_specs=[anywhere] * 7,
        out_specs=anywhere,
        scratch_shapes=[
            pltpu.SMEM(skeleton.shape, jnp.int32),
            pltpu.VMEM((tiles, tile), jnp.int32),
            pltpu.VMEM(linear_table.shape, F32),
            pltpu.VMEM(cubic_table.shape, F32),
            pltpu.VMEM((parts, rows, wide), BF16),
            pltpu.VMEM((tiles, tile, rank), BF16),
            pltpu.VMEM(transfer.shape, BF16),
            pltpu.VMEM((tiles, rank, tile), BF16),
            pltpu.VMEM((rank, rows), BF16),
            pltpu.VMEM((rank, rows), BF16),
            pltpu.VMEM((levels, 2 * rank, rank), BF16),
            pltpu.VMEM((rows, columns), F32),
            pltpu.VMEM((rows, columns), F32),
            pltpu.VMEM((parts, rows, wide), BF16),
            pltpu.VMEM((2, parts, n, share, rank), F32),
            pltpu.VMEM((2, parts, n, share, rank), BF16),
            pltpu.VMEM((2, parts, n - 1, share, rank), BF16),
            pltpu.VMEM((2, levels, parts, share, rank), BF16),
            pltpu.VMEM((2, levels, parts, share, rank), BF16),
            pltpu.VMEM((2, parts, share, rank), BF16),
            pltpu.VMEM((parts, n, share, rank), BF16),
            dma((4,)),
            dma((parts,)),
            dma((2 + parts,)),
            dma((2, parts, n - 1)),
            dma((2, parts, n - 1)),
            dma((2, levels, parts)),
            dma((2, levels, parts)),
            dma((2, parts, n - 1)),
            dma((2, parts, n - 1)),
        ],
        compiler_params=pltpu.CompilerParams(
            collective_id=0, has_side_effects=True, vmem_limit_bytes=67043328
        ),
        name="butterfly",
    )(
        skeleton,
        row_class.reshape(tiles, tile),
        linear_table,
        cubic_table,
        source,
        basis.reshape(tiles, tile, rank),
        transfer,
    )
    adjoint = pl.pallas_call(
        functools.partial(expand_kernel, tiles, tile, rho),
        out_shape=jax.ShapeDtypeStruct((tiles, tile, columns), BF16),
        in_specs=[anywhere] * 3,
        out_specs=anywhere,
        scratch_shapes=[
            pltpu.SMEM(skeleton.shape, jnp.int32),
            pltpu.VMEM(basis.shape, BF16),
            pltpu.VMEM((columns, rank), BF16),
            pltpu.VMEM((tiles, tile, columns), BF16),
            dma((3,)),
            dma((tiles,)),
        ],
        compiler_params=pltpu.CompilerParams(vmem_limit_bytes=67043328),
        name="expand",
    )(skeleton, basis, returned.reshape(columns, rank))
    return adjoint.reshape(rows, columns)


def solution(mesh):
    placed = (
        P(("ens", "bfly", "cblk"), None),
        P(("ens", "bfly", "cblk"), None),
        P("ens", "bfly", None, None),
        P(("ens", "bfly", "cblk"), None),
        P(("ens", "bfly", "cblk")),
        P(),
        P(),
    )
    return jax.shard_map(
        per_device,
        mesh=mesh,
        in_specs=placed,
        out_specs=P(("ens", "bfly", "cblk"), None),
        check_vma=False,
    )
```
